32 devices in a mesh: path: 2 (over x), mesh: 2 (over y), grid: 8 (over z, core).
Axes of the slice: x: 2, y: 2, z: 4, core: 2. Of those that a mesh axis runs over, the one named last changes fastest.
Arguments:
- path_bands: float32 [2, 16, 64, 64, 128], P('path', None, 'grid'), may hold values from -6 to 6
- occupied: float32 [2, 1, 64, 64, 128], P('mesh', None, 'grid', 'path'), may hold values from -6 to 6
- path_kpts: int32 [2, 3], P('path'), may hold values from 0 to 7
- mesh_kpts: int32 [2, 3], replicated, may hold values from 0 to 7
- mesh_shift: int32 [2, 3], replicated, may hold values from -1 to 1
Outputs:
- applied: float32 [2, 16, 64, 64, 128], P('path', 'mesh', 'grid')
- intersection: float32 [2, 2, 16, 16], P('path')
The draws below stay inside these ranges and needn't reach their ends.
All inputs are finite; a program needn't handle non-finite values.
Results may differ from the reference program's by a relative error of at most 0.0001.
Values sent between devices are 32-bit elements; how exact they have to be, the bound alone decides.
No kernel may reach another device: no remote copies, remote signals or barrier semaphores. Data moves between devices by JAX's collectives and lax.ppermute only.
A program may use at most 64 MiB of HBM per device.

```python
import math
import jax
import jax.numpy as jnp
from jax import lax

NG = 64
NB = 16
NOCC = 1
KDIV = 8
NK = 2
NQ = 2


def plant(result, rng, least, largest):
    longest = result.shape.index(max(result.shape))
    spots = []
    for shift in (0, 1):
        where = [jax.random.randint(jax.random.fold_in(rng, axis), (), 0, length) for axis, length in enumerate(result.shape)]
        where[longest] = (where[longest] + shift) % result.shape[longest]
        spots.append(tuple(where))
    return result.at[spots[0]].set(least).at[spots[1]].set(largest)


def steps_of(stream_key, dims, shards, smallest, high):
    loudness, own = 1.0, jax.random.fold_in(stream_key, 6)
    for axis_at, parts in shards:
        steps = jnp.exp(jax.random.uniform(jax.random.fold_in(own, axis_at), (parts,), jnp.float32, smallest / len(shards), high / len(shards)))
        loudness = loudness * jnp.repeat(steps, dims[axis_at] // parts).reshape([-1 if axis == axis_at else 1 for axis in range(len(dims))])
    return loudness


def noise(rng, shape, spread, bound, split=(), kind=jnp.bfloat16):
    gain = steps_of(rng, shape, split, -0.22, 0.18) if split else 1.0
    entries = jax.random.normal(rng, shape, jnp.float32) * spread * gain
    return jnp.minimum(jnp.maximum(entries, -bound), bound).astype(kind)


def setup_inputs(seed: int = 0) -> dict:
    key_list = jax.random.split(jax.random.key(seed), 6)
    path_bands = noise(key_list[0], (NK, NB, NG, NG, 2 * NG), 1.0, 6.0, ((0, 2), (2, 8)), jnp.float32)
    occupied = noise(key_list[1], (NQ, NOCC, NG, NG, 2 * NG), 1.0, 6.0, ((0, 2), (2, 8), (3, 2)), jnp.float32)
    path_kpts = plant(jax.random.randint(key_list[2], (NK, 3), 0, KDIV), jax.random.fold_in(key_list[2], 1), 0, KDIV - 1).astype(jnp.int32)
    mesh_kpts = plant(jax.random.randint(key_list[3], (NQ, 3), 0, KDIV), jax.random.fold_in(key_list[3], 1), 0, KDIV - 1).astype(jnp.int32)
    mesh_shift = plant(jax.random.randint(key_list[4], (NQ, 3), -1, 2), jax.random.fold_in(key_list[4], 1), -1, 1).astype(jnp.int32)
    return {"path_bands": path_bands, "occupied": occupied, "path_kpts": path_kpts, "mesh_kpts": mesh_kpts, "mesh_shift": mesh_shift}


BOX_LENGTH = 42.7
SCREEN_SQ = 0.04
MIXING = 0.25
HIGHEST_PRECISION = lax.Precision.HIGHEST


def signed_frequencies(points):
    indices = jnp.arange(points, dtype=jnp.int32)
    return (indices + points // 2) % points - points // 2


def screened_coulomb(offset_frac):
    freqs = signed_frequencies(NG).astype(jnp.float32)
    squares = ((freqs + offset_frac[0]) ** 2)[:, None, None] + ((freqs + offset_frac[1]) ** 2)[None, :, None] + ((freqs + offset_frac[2]) ** 2)[None, None, :]
    return 4.0 * math.pi / ((2.0 * math.pi / BOX_LENGTH) ** 2 * squares + SCREEN_SQ)


def twist_phase(shift):
    coords = jnp.arange(NG, dtype=jnp.int32)
    product = (shift[0] * coords[:, None, None] + shift[1] * coords[None, :, None] + shift[2] * coords[None, None, :]) % NG
    angles = (2.0 * math.pi / NG) * product.astype(jnp.float32)
    return lax.complex(jnp.cos(angles), jnp.sin(angles))


def as_complex(values):
    return lax.complex(values[..., :NG], values[..., NG:])


def reference(path_bands, occupied, path_kpts, mesh_kpts, mesh_shift):
    rotated = [as_complex(occupied[mesh_point]) * twist_phase(mesh_shift[mesh_point]) for mesh_point in range(NQ)]

    def one_point(inputs):
        band_values, kpoint = inputs
        bands_complex = as_complex(band_values)
        applied = jnp.zeros_like(bands_complex)
        for mesh_point in range(NQ):
            offset_frac = (kpoint - mesh_kpts[mesh_point]).astype(jnp.float32) / KDIV
            kernel = screened_coulomb(offset_frac)
            orbitals = rotated[mesh_point]
            pair_density = jnp.conj(orbitals)[:, None] * bands_complex[None]
            potential = jnp.fft.ifftn(jnp.fft.fftn(pair_density, axes=(2, 3, 4)) * kernel, axes=(2, 3, 4))
            applied = applied - MIXING * jnp.sum(orbitals[:, None] * potential, axis=0)
        intersection = jnp.einsum("axyz,bxyz->ab", jnp.conj(bands_complex), applied, precision=HIGHEST_PRECISION) / NG ** 3
        return (jnp.concatenate([applied.real, applied.imag], -1), jnp.stack([intersection.real, intersection.imag]))

    applied_all, intersection_all = lax.map(one_point, (path_bands, path_kpts))
    return applied_all, intersection_all
```

```python
import math

import jax
import jax.numpy as jnp
import ml_dtypes
import numpy as np
from jax import lax
from jax.experimental import pallas as pl
from jax.experimental.pallas import tpu as pltpu
from jax.sharding import PartitionSpec as P

KDIV = 8


BOX_LENGTH = 42.7
SCREEN_SQ = 0.04
MIXING = 0.25
HIGHEST_PRECISION = lax.Precision.HIGHEST


def signed_frequencies(indices, points):
    return (indices + points // 2) % points - points // 2


def dft_tables(positions, points):
    freqs = jnp.arange(points, dtype=jnp.int32)
    product = positions[:, None] * freqs[None, :] % points
    angles = 2.0 * math.pi / points * product.astype(jnp.float32)
    return (jnp.cos(angles), jnp.sin(angles))


def last_matrix(points, inverse):
    cosine_table, sine_table = dft_tables(jnp.arange(points, dtype=jnp.int32), points)
    if inverse:
        upper = jnp.concatenate([cosine_table, sine_table], 1)
        lower = jnp.concatenate([-sine_table, cosine_table], 1)
    else:
        upper = jnp.concatenate([cosine_table, -sine_table], 1)
        lower = jnp.concatenate([sine_table, cosine_table], 1)
    return jnp.concatenate([upper, lower], 0)


def along_axis(values, cosine_table, sine_table, contract_dim, inverse):
    letters = "abcde"
    form = (
        letters
        + ","
        + letters[contract_dim]
        + "w->"
        + letters[:contract_dim]
        + "w"
        + letters[contract_dim + 1 :]
    )
    cos_part = jnp.einsum(form, values, cosine_table, precision=HIGHEST_PRECISION)
    sin_part = jnp.einsum(form, values, sine_table, precision=HIGHEST_PRECISION)
    half_width = values.shape[-1] // 2
    sin_real = sin_part[..., :half_width]
    sin_imag = sin_part[..., half_width:]
    if inverse:
        return cos_part + jnp.concatenate([-sin_imag, sin_real], -1)
    return cos_part + jnp.concatenate([sin_imag, -sin_real], -1)


def rotate_orbitals(orbitals, shifts, x_planes):
    points = orbitals.shape[3]
    coords = jnp.arange(points, dtype=jnp.int32)
    product = (
        shifts[:, 0][:, None, None, None] * x_planes[None, :, None, None]
        + shifts[:, 1][:, None, None, None] * coords[None, None, :, None]
        + shifts[:, 2][:, None, None, None] * coords[None, None, None, :]
    ) % points
    angles = 2.0 * math.pi / points * product.astype(jnp.float32)
    cosines = jnp.cos(angles)[:, None]
    sines = jnp.sin(angles)[:, None]
    real_part = orbitals[..., :points]
    imag_part = orbitals[..., points:]
    return jnp.concatenate(
        [real_part * cosines - imag_part * sines, real_part * sines + imag_part * cosines], -1
    )


def pair_fields(rotated, band_fields):
    points = band_fields.shape[2]
    rot_real = rotated[..., :points][:, :, None]
    rot_imag = rotated[..., points:][:, :, None]
    band_real = band_fields[..., :points][None, None]
    band_imag = band_fields[..., points:][None, None]
    pairs = jnp.concatenate(
        [rot_real * band_real + rot_imag * band_imag, rot_real * band_imag - rot_imag * band_real],
        -1,
    )
    return pairs.reshape(
        (rotated.shape[0], rotated.shape[1] * band_fields.shape[0]) + band_fields.shape[1:]
    )


def accumulate(rotated, potential, nbands):
    points = rotated.shape[3]
    shaped = potential.reshape((rotated.shape[0], rotated.shape[1], nbands) + potential.shape[2:])
    rot_real = rotated[..., :points][:, :, None]
    rot_imag = rotated[..., points:][:, :, None]
    pot_real = shaped[..., :points]
    pot_imag = shaped[..., points:]
    summed = jnp.concatenate(
        [
            jnp.sum(rot_real * pot_real - rot_imag * pot_imag, axis=(0, 1)),
            jnp.sum(rot_real * pot_imag + rot_imag * pot_real, axis=(0, 1)),
        ],
        -1,
    )
    return -MIXING * summed


def intersection_part(band_fields, applied):
    points = band_fields.shape[2]
    nbands = band_fields.shape[0]
    band_real = band_fields[..., :points].reshape(nbands, -1)
    band_imag = band_fields[..., points:].reshape(nbands, -1)
    app_real = applied[..., :points].reshape(applied.shape[0], -1)
    app_imag = applied[..., points:].reshape(applied.shape[0], -1)
    real_sum = jnp.dot(band_real, app_real.T, precision=HIGHEST_PRECISION) + jnp.dot(
        band_imag, app_imag.T, precision=HIGHEST_PRECISION
    )
    imag_sum = jnp.dot(band_real, app_imag.T, precision=HIGHEST_PRECISION) - jnp.dot(
        band_imag, app_real.T, precision=HIGHEST_PRECISION
    )
    return jnp.stack([real_sum, imag_sum]) / float(points**3)


def screened_kernel(path_point, mesh_points, y_rows, points):
    offset_frac = (path_point[None, :] - mesh_points).astype(jnp.float32) / KDIV
    all_freqs = signed_frequencies(jnp.arange(points, dtype=jnp.int32), points).astype(jnp.float32)
    row_freqs = signed_frequencies(y_rows, points).astype(jnp.float32)
    square_x = (all_freqs[None, :] + offset_frac[:, 0:1]) ** 2
    square_y = (row_freqs[None, :] + offset_frac[:, 1:2]) ** 2
    square_z = (all_freqs[None, :] + offset_frac[:, 2:3]) ** 2
    squares = square_x[:, :, None, None] + square_y[:, None, :, None] + square_z[:, None, None, :]
    kernel = (
        4.0 * math.pi / ((2.0 * math.pi / BOX_LENGTH) ** 2 * squares + SCREEN_SQ) / float(points**3)
    )
    return jnp.concatenate([kernel, kernel], -1)


def spread_per_device(path_bands, occupied, path_kpts, mesh_kpts, mesh_shift):
    points = path_bands.shape[3]
    nbands = path_bands.shape[1]
    local_planes = path_bands.shape[2]
    grid_count = lax.axis_size("grid")
    mesh_count = lax.axis_size("mesh")
    grid_index = lax.axis_index("grid")
    mesh_index = lax.axis_index("mesh")
    whole_orbitals = lax.all_gather(occupied, "path", axis=3, tiled=True)
    forward_z = last_matrix(points, False)
    inverse_z = last_matrix(points, True)
    cos_y, sin_y = dft_tables(jnp.arange(points, dtype=jnp.int32), points)
    band_all = path_bands[0]
    path_point = path_kpts[0]
    share_planes = local_planes // mesh_count
    both_orbitals = lax.all_to_all(whole_orbitals, "mesh", split_axis=2, concat_axis=0, tiled=True)
    x_planes = (
        grid_index * local_planes
        + mesh_index * share_planes
        + jnp.arange(share_planes, dtype=jnp.int32)
    )
    rotated = rotate_orbitals(both_orbitals, mesh_shift, x_planes)
    band_mine = lax.dynamic_slice_in_dim(band_all, mesh_index * share_planes, share_planes, 1)
    values = pair_fields(rotated, band_mine)
    values = jnp.matmul(values, forward_z, precision=HIGHEST_PRECISION)
    pair_field = along_axis(values, cos_y, sin_y, 3, False)
    wide_count = mesh_count * grid_count
    rows_y = points // wide_count
    flat_index = mesh_index * grid_count + grid_index
    y_rows = flat_index * rows_y + jnp.arange(rows_y, dtype=jnp.int32)
    kernel = screened_kernel(path_point, mesh_kpts, y_rows, points)
    positions = jnp.arange(points, dtype=jnp.int32)
    piece_index = positions // share_planes
    plane_index = (
        piece_index % grid_count * local_planes
        + piece_index // grid_count * share_planes
        + positions % share_planes
    )
    cos_x, sin_x = dft_tables(plane_index, points)
    moved = (
        along_axis(
            lax.all_to_all(pair_field, ("mesh", "grid"), split_axis=3, concat_axis=2, tiled=True),
            cos_x,
            sin_x,
            2,
            False,
        )
        * kernel[:, None]
    )
    moved = along_axis(moved, cos_x.T, sin_x.T, 2, True)
    potential = lax.all_to_all(moved, ("mesh", "grid"), split_axis=2, concat_axis=3, tiled=True)
    values = potential
    values = along_axis(values, cos_y, sin_y, 3, True)
    applied = accumulate(
        rotated, jnp.matmul(values, inverse_z, precision=HIGHEST_PRECISION), nbands
    )
    partial_value = intersection_part(band_mine, applied)
    result_bands = lax.all_to_all(applied, "mesh", split_axis=0, concat_axis=1, tiled=True)
    intersection = lax.psum(partial_value, ("mesh", "grid"))
    return (result_bands[None], intersection[None])


def split_table(table):
    high = table.astype(ml_dtypes.bfloat16)
    low = (table - high.astype(np.float64)).astype(ml_dtypes.bfloat16)
    return high, low

def transform_tables(points):
    index = np.arange(points)
    angles = 2.0 * np.pi * ((index[:, None] * index[None, :]) % points) / points
    cos, sin = np.cos(angles), np.sin(angles)
    zero = np.zeros_like(cos)
    last_forward = np.block([[cos, zero, -sin, zero], [sin, zero, cos, zero], [zero, cos, zero, -sin], [zero, sin, zero, cos]])
    last_inverse = np.block([[cos, sin, zero, zero], [zero, zero, cos, sin], [-sin, cos, zero, zero], [zero, zero, -sin, cos]])
    row_forward = np.block([[cos, sin], [-sin, cos]])
    row_inverse = np.block([[cos, -sin], [sin, cos]])
    last = []
    for table in (last_forward, last_inverse):
        last.extend(split_table(table))
    rows = []
    for table in (row_forward, row_inverse):
        high, low = split_table(table)
        rows.append(np.block([[high, high], [low, np.zeros_like(low)]]).astype(ml_dtypes.bfloat16))
    half = points // 2
    turn = 2.0 * np.pi * np.arange(half) / points
    ones = np.ones((half, points))
    twiddle = np.stack([np.concatenate([ones, ones * np.cos(turn)[:, None]], 1), np.concatenate([0 * ones, ones * np.sin(turn)[:, None]], 1)])
    return last, rows, twiddle.astype(np.float32)

def split_values(values):
    high = values.astype(jnp.bfloat16)
    low = (values - high.astype(jnp.float32)).astype(jnp.bfloat16)
    return high, low

def fft_list(real, imag):
    size = len(real)
    if size == 1:
        return real, imag
    half = size // 2
    even_r, even_i = fft_list(real[0::2], imag[0::2])
    odd_r, odd_i = fft_list(real[1::2], imag[1::2])
    out_r, out_i = [None] * size, [None] * size
    root = math.sqrt(0.5)
    for k in range(half):
        r, i = odd_r[k], odd_i[k]
        if k == 0:
            tr, ti = r, i
        elif 4 * k == size:
            tr, ti = i, -r
        elif 8 * k == size:
            tr, ti = (r + i) * root, (i - r) * root
        elif 8 * k == 3 * size:
            tr, ti = (i - r) * root, (r + i) * (-root)
        else:
            c, s = math.cos(2 * math.pi * k / size), math.sin(2 * math.pi * k / size)
            tr, ti = r * c + i * s, i * c - r * s
        if 4 * k == size:
            out_r[k], out_i[k] = even_r[k] + i, even_i[k] - r
            out_r[k + half], out_i[k + half] = even_r[k] - i, even_i[k] + r
        else:
            out_r[k], out_i[k] = even_r[k] + tr, even_i[k] + ti
            out_r[k + half], out_i[k + half] = even_r[k] - tr, even_i[k] - ti
    return out_r, out_i

def f32dot(a, b):
    return jnp.dot(a, b, preferred_element_type=jnp.float32)

def pair_kernel(core_ref, mine_ref, other_ref, rot_ref, kern_ref, lfh, lfl, lih, lil, rf, ri, tw_ref, keep_ref, send_ref, vre, vim):
    nz, share, rows, lanes = mine_ref.shape
    points = rows
    half_z = nz // 2
    core = core_ref[0]
    low = lax.broadcasted_iota(jnp.int32, (rows, lanes), 1) < points

    def swap(v):
        return pltpu.roll(v, points, v.ndim - 1)

    def rotated(x):
        r = rot_ref[x]
        s = swap(r)
        return jnp.where(low, r, s), jnp.where(low, s, -r)

    step = 4
    def forward(src_ref, parity, zz, part):
        first = 2 * share * zz + share * parity + part * step
        halves = []
        for upper in (0, 1):
            planes = []
            for i in range(step):
                x = first + i + upper * half_z * 2 * share
                rr, rim = rotated(x)
                band = src_ref[zz + upper * half_z, part * step + i]
                planes.append(rr * band + rim * swap(band))
            halves.append(jnp.concatenate(planes, 0))
        values = jnp.concatenate(halves, 1)
        hi, lo = split_values(values)
        u = f32dot(hi, lfh[...]) + f32dot(lo, lfh[...]) + f32dot(hi, lfl[...])
        uh, ul = split_values(u)
        for i in range(0, step, 2):
            def stack(v):
                cols = [jnp.concatenate([v[(i + j) * rows:(i + j + 1) * rows, :lanes], v[(i + j) * rows:(i + j + 1) * rows, lanes:]], 0) for j in (0, 1)]
                return jnp.concatenate(cols, 1)
            d = f32dot(rf[...], jnp.concatenate([stack(uh), stack(ul)], 0))
            v = d[:2 * rows] + d[2 * rows:]
            for j in (0, 1):
                vre[first + i + j] = v[:rows, j * lanes:(j + 1) * lanes]
                vim[first + i + j] = v[rows:, j * lanes:(j + 1) * lanes]

    def inverse(parity, out_ref, zz, part):
        first = 2 * share * zz + share * parity + part * step
        res = []
        for i in range(0, step, 2):
            parts = [[], []]
            for j in (0, 1):
                for p, ref in enumerate((vre, vim)):
                    h, l = split_values(ref[first + i + j])
                    parts[j].append((h, l))
            cols = [jnp.concatenate([q[0][0], q[1][0], q[0][1], q[1][1]], 0) for q in parts]
            d = f32dot(ri[...], jnp.concatenate(cols, 1))
            u = d[:2 * rows] + d[2 * rows:]
            for j in (0, 1):
                res.append(jnp.concatenate([u[:rows, j * lanes:(j + 1) * lanes], u[rows:, j * lanes:(j + 1) * lanes]], 1))
        values = jnp.concatenate(res, 0)
        hi, lo = split_values(values)
        p = f32dot(hi, lih[...]) + f32dot(lo, lih[...]) + f32dot(hi, lil[...])
        for i in range(step):
            for upper in (0, 1):
                x = first + i + upper * half_z * 2 * share
                rr, rim = rotated(x)
                pot = p[i * rows:(i + 1) * rows, upper * lanes:(upper + 1) * lanes]
                out_ref[zz + upper * half_z, part * step + i] = rr * pot - rim * swap(pot)

    parts = share // step
    def fwd_body(t, carry):
        zz, part = t // parts, t % parts
        forward(mine_ref, core, zz, part)
        forward(other_ref, 1 - core, zz, part)
        return carry
    lax.fori_loop(0, half_z * parts, fwd_body, 0)

    n = vre.shape[0]
    sub = 8
    sign = jnp.where(low[:sub], 1.0, -1.0).astype(jnp.float32)
    def x_body(t, carry):
        sl = pl.ds(pl.multiple_of(t * sub, sub), sub)
        re, im = [], []
        for x in range(n):
            a, b = vre[x, sl, :], vim[x, sl, :]
            a = a * sign + swap(a)
            b = b * sign + swap(b)
            if x:
                c, s = tw_ref[0, x:x + 1, :], tw_ref[1, x:x + 1, :]
                a, b = a * c + b * s, b * c - a * s
            re.append(a); im.append(b)
        re, im = fft_list(re, im)
        for x in range(n):
            k = kern_ref[x, sl, :]
            re[x] = re[x] * k
            im[x] = im[x] * k
        im, re = fft_list(im, re)
        for x in range(n):
            a, b = re[x], im[x]
            if x:
                c, s = tw_ref[0, x:x + 1, :], tw_ref[1, x:x + 1, :]
                a, b = a * c - b * s, b * c + a * s
            vre[x, sl, :] = a * sign + swap(a)
            vim[x, sl, :] = b * sign + swap(b)
        return carry
    lax.fori_loop(0, rows // sub, x_body, 0)

    def inv_body(t, carry):
        zz, part = t // parts, t % parts
        inverse(core, keep_ref, zz, part)
        inverse(1 - core, send_ref, zz, part)
        return carry
    lax.fori_loop(0, half_z * parts, inv_body, 0)

def apply_pair(core, mine, other, rot, kern):
    nz, share, rows, lanes = mine.shape
    last, row, tw = transform_tables(rows)
    shape = jax.ShapeDtypeStruct(mine.shape, jnp.float32)
    vm = pl.BlockSpec(memory_space=pltpu.VMEM)
    n = nz * share
    return pl.pallas_call(
        pair_kernel,
        out_shape=(shape, shape),
        in_specs=[pl.BlockSpec(memory_space=pltpu.SMEM)] + [vm] * 11,
        out_specs=(vm, vm),
        scratch_shapes=[pltpu.VMEM((n, rows, lanes), jnp.float32)] * 2,
        cost_estimate=pl.CostEstimate(flops=2 * 10**9, bytes_accessed=7 * 2**20, transcendentals=0),
        compiler_params=pltpu.CompilerParams(vmem_limit_bytes=40 * 2**20),
        name="pair",
    )(core, mine, other, rot, kern, *[jnp.asarray(t) for t in last], *[jnp.asarray(t) for t in row], jnp.asarray(tw))


LANES = 128


def intersect_kernel(slot_ref, bands_ref, a0, a1, a2, a3, before_ref, out_ref, turned, sums):
    chunks = (a0, a1, a2, a3)
    nbands, cells, lanes = bands_ref.shape
    sub, group = 8, 4
    low = lax.broadcasted_iota(jnp.int32, (cells, lanes), 1) < lanes // 2
    for d, chunk in enumerate(chunks):
        value = chunk[...]
        rolled = pltpu.roll(value, lanes // 2, 1)
        turned[d] = jnp.where(low, rolled, -rolled)
    for first in range(0, nbands, group):

        def body(t, acc):
            sl = pl.ds(pl.multiple_of(t * sub, sub), sub)
            bands = [bands_ref[first + a, sl, :] for a in range(group)]
            out = []
            for d in range(len(chunks)):
                real, imag = chunks[d][sl, :], turned[d, sl, :]
                for a in range(group):
                    at = 2 * (d * group + a)
                    out.append(acc[at] + bands[a] * real)
                    out.append(acc[at + 1] + bands[a] * imag)
            return tuple(out)

        zero = jnp.zeros((sub, lanes), jnp.float32)
        acc = lax.fori_loop(0, cells // sub, body, (zero,) * (2 * group * len(chunks)), unroll=2)
        for d in range(len(chunks)):
            for a in range(group):
                at = 2 * (d * group + a)
                sums[d, first + a] = acc[at]
                sums[d, nbands + first + a] = acc[at + 1]
    column = lax.broadcasted_iota(jnp.int32, out_ref.shape, 1)
    total = before_ref[...]
    for d in range(len(chunks)):
        value = jnp.sum(jnp.sum(sums[d], axis=1), axis=1, keepdims=True)
        total = total + jnp.where(column == slot_ref[d], value, 0.0)
    out_ref[...] = total


def intersect(slots, bands, chunks, before):
    nbands, lanes = bands.shape[0], bands.shape[-1]
    bands = bands.reshape(nbands, -1, lanes)
    chunks = [chunk.reshape(-1, lanes) for chunk in chunks]
    cells = bands.shape[1]
    vm = pl.BlockSpec(memory_space=pltpu.VMEM)
    return pl.pallas_call(
        intersect_kernel,
        out_shape=jax.ShapeDtypeStruct((2 * nbands, lanes), jnp.float32),
        in_specs=[pl.BlockSpec(memory_space=pltpu.SMEM)] + [vm] * 6,
        out_specs=vm,
        scratch_shapes=[
            pltpu.VMEM((4, cells, lanes), jnp.float32),
            pltpu.VMEM((4, 2 * nbands, 8, lanes), jnp.float32),
        ],
        cost_estimate=pl.CostEstimate(flops=10**7, bytes_accessed=5 * 2**20, transcendentals=0),
        compiler_params=pltpu.CompilerParams(vmem_limit_bytes=24 * 2**20),
        name="intersect",
    )(slots, bands, *chunks, before)


def owner_kernel_values(path_point, mesh_point, shift, points):
    half = points // 2
    offset = (path_point - mesh_point).astype(jnp.float32) / KDIV
    lane = jnp.arange(2 * points, dtype=jnp.int32)

    def square(indices, axis):
        freqs = signed_frequencies(indices - shift[axis], points).astype(jnp.float32)
        return (freqs + offset[axis]) ** 2

    x_index = 2 * jnp.arange(half, dtype=jnp.int32)[:, None] + lane[None, :] // points
    plane = square(x_index, 0) + square(lane % points, 2)[None, :]
    rows = square(jnp.arange(points, dtype=jnp.int32), 1)
    squares = plane[:, None, :] + rows[None, :, None]
    scale = -MIXING * 4.0 * math.pi / float(points**3)
    return scale / ((2.0 * math.pi / BOX_LENGTH) ** 2 * squares + SCREEN_SQ)


def owner_per_device(path_bands, occupied, path_kpts, mesh_kpts, mesh_shift):
    points = path_bands.shape[3]
    nbands = path_bands.shape[1]
    share = path_bands.shape[2]
    grid_count = lax.axis_size("grid")
    mesh_count = lax.axis_size("mesh")
    path_count = lax.axis_size("path")
    grid_index = lax.axis_index("grid")
    mesh_index = lax.axis_index("mesh")
    path_index = lax.axis_index("path")
    core = grid_index % 2
    z = grid_index // 2
    nz = grid_count // 2
    column_bands = nbands // mesh_count
    rounds = column_bands // nz
    bands = path_bands[0]
    offsets = [d for d in (2, 3, 1)]

    def grid_swap(value, mask):
        return lax.ppermute(value, "grid", [(i, i ^ mask) for i in range(grid_count)])

    def axis_swap(value, axis, count):
        return lax.ppermute(value, axis, [(i, i ^ 1) for i in range(count)])

    def place(pieces):
        out = jnp.zeros((nz,) + pieces[0].shape, jnp.float32)
        for d, piece in enumerate(pieces):
            out = lax.dynamic_update_index_in_dim(out, piece, z ^ d, 0)
        return out

    piece = occupied[0, 0]
    got = {0: piece}
    for d in offsets:
        got[d] = grid_swap(piece, 2 * d)

    received = []
    for turn in range(rounds):
        parts = {}
        for d in [0] + offsets:
            at = mesh_index * column_bands + rounds * (z ^ d) + turn
            sent = lax.dynamic_index_in_dim(bands, at, 0, keepdims=False)
            parts[d] = sent if d == 0 else grid_swap(sent, 2 * d)
        received.append(parts)

    planes = place([got[d] for d in range(nz)])
    first, second = planes[: nz // 2], planes[nz // 2 :]
    same = mesh_index == core

    def by_rows(mine):
        theirs = axis_swap(mine, "path", path_count)
        low = path_index == 0
        return jnp.concatenate([jnp.where(low, mine, theirs), jnp.where(low, theirs, mine)], -2)

    def by_orbital(mine):
        theirs = axis_swap(mine, "mesh", mesh_count)
        kept = jnp.where(same, mine, theirs)
        crossed = grid_swap(jnp.where(same, theirs, mine), 1)
        low = core == 0
        return jnp.stack([jnp.where(low, kept, crossed), jnp.where(low, crossed, kept)], 1)

    orbital = jnp.concatenate([by_rows(by_orbital(first)), by_orbital(by_rows(second))], 0)
    orbital = orbital.reshape(points, points, 2 * points)

    mesh_point = lax.dynamic_index_in_dim(mesh_kpts, core, 0, keepdims=False)
    shift = lax.dynamic_index_in_dim(mesh_shift, core, 0, keepdims=False)
    kernel = owner_kernel_values(path_kpts[0], mesh_point, shift, points)
    core_word = core.reshape(1)
    result = jnp.zeros((column_bands, share, points, 2 * points), jnp.float32)
    inner = jnp.zeros((2 * nbands, 2 * points), jnp.float32)
    for turn in range(rounds):
        mine = place([received[turn][d] for d in range(nz)])
        other = grid_swap(mine, 1)
        keep, send = apply_pair(core_word, mine, other, orbital, kernel)
        total = keep + grid_swap(send, 1)
        chunks = {}
        for d in [0] + offsets:
            chunk = lax.dynamic_index_in_dim(total, z ^ d, 0, keepdims=False)
            chunks[d] = chunk if d == 0 else grid_swap(chunk, 2 * d)
        slots = jnp.stack([rounds * (z ^ d) + turn for d in range(nz)])
        for d in range(nz):
            result = lax.dynamic_update_index_in_dim(result, chunks[d], rounds * (z ^ d) + turn, 0)
        inner = intersect(
            mesh_index * column_bands + slots, bands, [chunks[d] for d in range(nz)], inner
        )
    for mask in [1 << b for b in range(grid_count.bit_length() - 1)]:
        inner = inner + grid_swap(inner, mask)
    inner = inner + axis_swap(inner, "mesh", mesh_count)
    intersection = inner[:, :nbands].reshape(2, nbands, nbands) / float(points**3)
    return (result[None], intersection[None])


def owner_fits(mesh, path_bands, occupied):
    paths, columns, planes = mesh.shape["path"], mesh.shape["mesh"], mesh.shape["grid"]
    points, nbands = path_bands.shape[3], path_bands.shape[1]
    orbitals = occupied.shape[0] * occupied.shape[1]
    return (
        paths == 2
        and columns == 2
        and planes == 8
        and path_bands.shape[0] == paths
        and occupied.shape[0] == columns
        and orbitals == columns
        and 2 * points == LANES
        and path_bands.shape[2] == points
        and nbands % (columns * planes // 2) == 0
        and points % (4 * planes) == 0
    )


def solution(mesh):
    def run(path_bands, occupied, path_kpts, mesh_kpts, mesh_shift):
        fits = owner_fits(mesh, path_bands, occupied)
        return jax.shard_map(
            owner_per_device if fits else spread_per_device,
            mesh=mesh,
            in_specs=(
                P("path", None, "grid", None, None),
                P("mesh", None, "grid", "path", None),
                P("path", None),
                P(),
                P(),
            ),
            out_specs=(P("path", "mesh", "grid", None, None), P("path", None, None, None)),
            check_vma=False,
        )(path_bands, occupied, path_kpts, mesh_kpts, mesh_shift)

    return run
```

```python
import math

import jax
import jax.numpy as jnp
import ml_dtypes
import numpy as np
from jax import lax
from jax.experimental import pallas as pl
from jax.experimental.pallas import tpu as pltpu
from jax.sharding import PartitionSpec as P

KDIV = 8


BOX_LENGTH = 42.7
SCREEN_SQ = 0.04
MIXING = 0.25
HIGHEST_PRECISION = lax.Precision.HIGHEST


def signed_frequencies(indices, points):
    return (indices + points // 2) % points - points // 2


def dft_tables(positions, points):
    freqs = jnp.arange(points, dtype=jnp.int32)
    product = positions[:, None] * freqs[None, :] % points
    angles = 2.0 * math.pi / points * product.astype(jnp.float32)
    return (jnp.cos(angles), jnp.sin(angles))


def last_matrix(points, inverse):
    cosine_table, sine_table = dft_tables(jnp.arange(points, dtype=jnp.int32), points)
    if inverse:
        upper = jnp.concatenate([cosine_table, sine_table], 1)
        lower = jnp.concatenate([-sine_table, cosine_table], 1)
    else:
        upper = jnp.concatenate([cosine_table, -sine_table], 1)
        lower = jnp.concatenate([sine_table, cosine_table], 1)
    return jnp.concatenate([upper, lower], 0)


def along_axis(values, cosine_table, sine_table, contract_dim, inverse):
    letters = "abcde"
    form = (
        letters
        + ","
        + letters[contract_dim]
        + "w->"
        + letters[:contract_dim]
        + "w"
        + letters[contract_dim + 1 :]
    )
    cos_part = jnp.einsum(form, values, cosine_table, precision=HIGHEST_PRECISION)
    sin_part = jnp.einsum(form, values, sine_table, precision=HIGHEST_PRECISION)
    half_width = values.shape[-1] // 2
    sin_real = sin_part[..., :half_width]
    sin_imag = sin_part[..., half_width:]
    if inverse:
        return cos_part + jnp.concatenate([-sin_imag, sin_real], -1)
    return cos_part + jnp.concatenate([sin_imag, -sin_real], -1)


def rotate_orbitals(orbitals, shifts, x_planes):
    points = orbitals.shape[3]
    coords = jnp.arange(points, dtype=jnp.int32)
    product = (
        shifts[:, 0][:, None, None, None] * x_planes[None, :, None, None]
        + shifts[:, 1][:, None, None, None] * coords[None, None, :, None]
        + shifts[:, 2][:, None, None, None] * coords[None, None, None, :]
    ) % points
    angles = 2.0 * math.pi / points * product.astype(jnp.float32)
    cosines = jnp.cos(angles)[:, None]
    sines = jnp.sin(angles)[:, None]
    real_part = orbitals[..., :points]
    imag_part = orbitals[..., points:]
    return jnp.concatenate(
        [real_part * cosines - imag_part * sines, real_part * sines + imag_part * cosines], -1
    )


def pair_fields(rotated, band_fields):
    points = band_fields.shape[2]
    rot_real = rotated[..., :points][:, :, None]
    rot_imag = rotated[..., points:][:, :, None]
    band_real = band_fields[..., :points][None, None]
    band_imag = band_fields[..., points:][None, None]
    pairs = jnp.concatenate(
        [rot_real * band_real + rot_imag * band_imag, rot_real * band_imag - rot_imag * band_real],
        -1,
    )
    return pairs.reshape(
        (rotated.shape[0], rotated.shape[1] * band_fields.shape[0]) + band_fields.shape[1:]
    )


def accumulate(rotated, potential, nbands):
    points = rotated.shape[3]
    shaped = potential.reshape((rotated.shape[0], rotated.shape[1], nbands) + potential.shape[2:])
    rot_real = rotated[..., :points][:, :, None]
    rot_imag = rotated[..., points:][:, :, None]
    pot_real = shaped[..., :points]
    pot_imag = shaped[..., points:]
    summed = jnp.concatenate(
        [
            jnp.sum(rot_real * pot_real - rot_imag * pot_imag, axis=(0, 1)),
            jnp.sum(rot_real * pot_imag + rot_imag * pot_real, axis=(0, 1)),
        ],
        -1,
    )
    return -MIXING * summed


def intersection_part(band_fields, applied):
    points = band_fields.shape[2]
    nbands = band_fields.shape[0]
    band_real = band_fields[..., :points].reshape(nbands, -1)
    band_imag = band_fields[..., points:].reshape(nbands, -1)
    app_real = applied[..., :points].reshape(applied.shape[0], -1)
    app_imag = applied[..., points:].reshape(applied.shape[0], -1)
    real_sum = jnp.dot(band_real, app_real.T, precision=HIGHEST_PRECISION) + jnp.dot(
        band_imag, app_imag.T, precision=HIGHEST_PRECISION
    )
    imag_sum = jnp.dot(band_real, app_imag.T, precision=HIGHEST_PRECISION) - jnp.dot(
        band_imag, app_real.T, precision=HIGHEST_PRECISION
    )
    return jnp.stack([real_sum, imag_sum]) / float(points**3)


def screened_kernel(path_point, mesh_points, y_rows, points):
    offset_frac = (path_point[None, :] - mesh_points).astype(jnp.float32) / KDIV
    all_freqs = signed_frequencies(jnp.arange(points, dtype=jnp.int32), points).astype(jnp.float32)
    row_freqs = signed_frequencies(y_rows, points).astype(jnp.float32)
    square_x = (all_freqs[None, :] + offset_frac[:, 0:1]) ** 2
    square_y = (row_freqs[None, :] + offset_frac[:, 1:2]) ** 2
    square_z = (all_freqs[None, :] + offset_frac[:, 2:3]) ** 2
    squares = square_x[:, :, None, None] + square_y[:, None, :, None] + square_z[:, None, None, :]
    kernel = (
        4.0 * math.pi / ((2.0 * math.pi / BOX_LENGTH) ** 2 * squares + SCREEN_SQ) / float(points**3)
    )
    return jnp.concatenate([kernel, kernel], -1)


def spread_per_device(path_bands, occupied, path_kpts, mesh_kpts, mesh_shift):
    points = path_bands.shape[3]
    nbands = path_bands.shape[1]
    local_planes = path_bands.shape[2]
    grid_count = lax.axis_size("grid")
    mesh_count = lax.axis_size("mesh")
    grid_index = lax.axis_index("grid")
    mesh_index = lax.axis_index("mesh")
    whole_orbitals = lax.all_gather(occupied, "path", axis=3, tiled=True)
    forward_z = last_matrix(points, False)
    inverse_z = last_matrix(points, True)
    cos_y, sin_y = dft_tables(jnp.arange(points, dtype=jnp.int32), points)
    band_all = path_bands[0]
    path_point = path_kpts[0]
    share_planes = local_planes // mesh_count
    both_orbitals = lax.all_to_all(whole_orbitals, "mesh", split_axis=2, concat_axis=0, tiled=True)
    x_planes = (
        grid_index * local_planes
        + mesh_index * share_planes
        + jnp.arange(share_planes, dtype=jnp.int32)
    )
    rotated = rotate_orbitals(both_orbitals, mesh_shift, x_planes)
    band_mine = lax.dynamic_slice_in_dim(band_all, mesh_index * share_planes, share_planes, 1)
    values = pair_fields(rotated, band_mine)
    values = jnp.matmul(values, forward_z, precision=HIGHEST_PRECISION)
    pair_field = along_axis(values, cos_y, sin_y, 3, False)
    wide_count = mesh_count * grid_count
    rows_y = points // wide_count
    flat_index = mesh_index * grid_count + grid_index
    y_rows = flat_index * rows_y + jnp.arange(rows_y, dtype=jnp.int32)
    kernel = screened_kernel(path_point, mesh_kpts, y_rows, points)
    positions = jnp.arange(points, dtype=jnp.int32)
    piece_index = positions // share_planes
    plane_index = (
        piece_index % grid_count * local_planes
        + piece_index // grid_count * share_planes
        + positions % share_planes
    )
    cos_x, sin_x = dft_tables(plane_index, points)
    moved = (
        along_axis(
            lax.all_to_all(pair_field, ("mesh", "grid"), split_axis=3, concat_axis=2, tiled=True),
            cos_x,
            sin_x,
            2,
            False,
        )
        * kernel[:, None]
    )
    moved = along_axis(moved, cos_x.T, sin_x.T, 2, True)
    potential = lax.all_to_all(moved, ("mesh", "grid"), split_axis=2, concat_axis=3, tiled=True)
    values = potential
    values = along_axis(values, cos_y, sin_y, 3, True)
    applied = accumulate(
        rotated, jnp.matmul(values, inverse_z, precision=HIGHEST_PRECISION), nbands
    )
    partial_value = intersection_part(band_mine, applied)
    result_bands = lax.all_to_all(applied, "mesh", split_axis=0, concat_axis=1, tiled=True)
    intersection = lax.psum(partial_value, ("mesh", "grid"))
    return (result_bands[None], intersection[None])


def split_table(table):
    high = table.astype(ml_dtypes.bfloat16)
    low = (table - high.astype(np.float64)).astype(ml_dtypes.bfloat16)
    return high, low


def transform_tables(points):
    index = np.arange(points)
    angles = 2.0 * np.pi * ((index[:, None] * index[None, :]) % points) / points
    cos, sin = np.cos(angles), np.sin(angles)
    zero = np.zeros_like(cos)
    last_forward = np.block([[cos, zero, -sin, zero], [sin, zero, cos, zero], [zero, cos, zero, -sin], [zero, sin, zero, cos]])
    last_inverse = np.block([[cos, sin, zero, zero], [zero, zero, cos, sin], [-sin, cos, zero, zero], [zero, zero, -sin, cos]])
    row_forward = np.block([[cos, sin], [-sin, cos]])
    row_inverse = np.block([[cos, -sin], [sin, cos]])
    last = []
    for table in (last_forward, last_inverse):
        last.extend(split_table(table))
    rows = []
    for table in (row_forward, row_inverse):
        high, low = split_table(table)
        rows.append(np.block([[high, high], [low, np.zeros_like(low)]]).astype(ml_dtypes.bfloat16))
    half = points // 2
    turn = 2.0 * np.pi * np.arange(half) / points
    ones = np.ones((half, points))
    twiddle = np.stack([np.concatenate([ones, ones * np.cos(turn)[:, None]], 1), np.concatenate([0 * ones, ones * np.sin(turn)[:, None]], 1)])
    return last, rows, twiddle.astype(np.float32)


def split_values(values):
    high = values.astype(jnp.bfloat16)
    low = (values - high.astype(jnp.float32)).astype(jnp.bfloat16)
    return high, low


def fft_list(real, imag):
    size = len(real)
    if size == 1:
        return real, imag
    half = size // 2
    even_r, even_i = fft_list(real[0::2], imag[0::2])
    odd_r, odd_i = fft_list(real[1::2], imag[1::2])
    out_r, out_i = [None] * size, [None] * size
    root = math.sqrt(0.5)
    for k in range(half):
        r, i = odd_r[k], odd_i[k]
        if k == 0:
            tr, ti = r, i
        elif 4 * k == size:
            tr, ti = i, -r
        elif 8 * k == size:
            tr, ti = (r + i) * root, (i - r) * root
        elif 8 * k == 3 * size:
            tr, ti = (i - r) * root, (r + i) * (-root)
        else:
            c, s = math.cos(2 * math.pi * k / size), math.sin(2 * math.pi * k / size)
            tr, ti = r * c + i * s, i * c - r * s
        if 4 * k == size:
            out_r[k], out_i[k] = even_r[k] + i, even_i[k] - r
            out_r[k + half], out_i[k + half] = even_r[k] - i, even_i[k] + r
        else:
            out_r[k], out_i[k] = even_r[k] + tr, even_i[k] + ti
            out_r[k + half], out_i[k + half] = even_r[k] - tr, even_i[k] - ti
    return out_r, out_i


def f32dot(a, b):
    return jnp.dot(a, b, preferred_element_type=jnp.float32)


def pair_kernel(spots_ref, *refs):
    nz = 4
    mine, other = refs[:nz], refs[nz : 2 * nz]
    first_own, first_far, second_kept, second_crossed = refs[2 * nz : 2 * nz + 4]
    kern_ref, table_ref, tw_ref = refs[2 * nz + 4 : 2 * nz + 7]
    lfh, lfl, lih, lil, rf, ri = [table_ref.at[at] for at in range(6)]
    keep, send = refs[2 * nz + 7 : 3 * nz + 7], refs[3 * nz + 7 : 4 * nz + 7]
    vre, vim = refs[4 * nz + 7 :]
    share, rows, lanes = mine[0].shape
    points = rows
    half_z = nz // 2
    z, core, path = spots_ref[0], spots_ref[1], spots_ref[2]
    low = lax.broadcasted_iota(jnp.int32, (rows, lanes), 1) < points
    step = 4

    def swap(v):
        return pltpu.roll(v, points, v.ndim - 1)

    def orbital(d, parity, i):
        if d < half_z:
            own, far = first_own[parity, d, i], first_far[parity, d, i]
        else:
            ref = second_crossed if parity else second_kept
            own, far = ref[0, d - half_z, i], ref[1, d - half_z, i]
        r = jnp.concatenate([jnp.where(path == 0, own, far), jnp.where(path == 0, far, own)], 0)
        s = swap(r)
        return jnp.where(low, r, s), jnp.where(low, s, -r)

    def place(d, parity, part):
        side = core if parity == 0 else 1 - core
        return share * (2 * ((z ^ d) & 1) + side) + part * step

    def forward(d, parity, part):
        first = place(d, parity, part)
        halves = []
        for at in (d, d ^ half_z):
            planes = []
            for i in range(step):
                real, imag = orbital(at, parity, part * step + i)
                band = (other if parity else mine)[at][part * step + i]
                planes.append(real * band + imag * swap(band))
            halves.append(jnp.concatenate(planes, 0))
        hi, lo = split_values(jnp.concatenate(halves, 1))
        u = f32dot(hi, lfh[...]) + f32dot(lo, lfh[...]) + f32dot(hi, lfl[...])
        uh, ul = split_values(u)
        for i in range(0, step, 2):

            def stack(v):
                cols = []
                for j in (0, 1):
                    plane = v[(i + j) * rows : (i + j + 1) * rows]
                    cols.append(jnp.concatenate([plane[:, :lanes], plane[:, lanes:]], 0))
                return jnp.concatenate(cols, 1)

            d2 = f32dot(rf[...], jnp.concatenate([stack(uh), stack(ul)], 0))
            v = d2[: 2 * rows] + d2[2 * rows :]
            for j in (0, 1):
                vre[first + i + j] = v[:rows, j * lanes : (j + 1) * lanes]
                vim[first + i + j] = v[rows:, j * lanes : (j + 1) * lanes]

    def inverse(d, parity, part):
        first = place(d, parity, part)
        res = []
        for i in range(0, step, 2):
            cols = []
            for j in (0, 1):
                rh, rl = split_values(vre[first + i + j])
                ih, il = split_values(vim[first + i + j])
                cols.append(jnp.concatenate([rh, ih, rl, il], 0))
            d2 = f32dot(ri[...], jnp.concatenate(cols, 1))
            u = d2[: 2 * rows] + d2[2 * rows :]
            for j in (0, 1):
                plane = u[:, j * lanes : (j + 1) * lanes]
                res.append(jnp.concatenate([plane[:rows], plane[rows:]], 1))
        hi, lo = split_values(jnp.concatenate(res, 0))
        p = f32dot(hi, lih[...]) + f32dot(lo, lih[...]) + f32dot(hi, lil[...])
        for i in range(step):
            for side, at in enumerate((d, d ^ half_z)):
                real, imag = orbital(at, parity, part * step + i)
                pot = p[i * rows : (i + 1) * rows, side * lanes : (side + 1) * lanes]
                out = send if parity else keep
                out[at][part * step + i] = real * pot - imag * swap(pot)

    def each_part(work):
        def body(part, carry):
            for d in range(half_z):
                for parity in (0, 1):
                    work(d, parity, part)
            return carry

        lax.fori_loop(0, share // step, body, 0)

    each_part(forward)

    n = vre.shape[0]
    sub = 8
    sign = jnp.where(low[:sub], 1.0, -1.0).astype(jnp.float32)

    def x_body(t, carry):
        sl = pl.ds(pl.multiple_of(t * sub, sub), sub)
        re, im = [], []
        for x in range(n):
            a, b = vre[x, sl, :], vim[x, sl, :]
            a = a * sign + swap(a)
            b = b * sign + swap(b)
            if x:
                c, s = tw_ref[0, x : x + 1, :], tw_ref[1, x : x + 1, :]
                a, b = a * c + b * s, b * c - a * s
            re.append(a)
            im.append(b)
        re, im = fft_list(re, im)
        for x in range(n):
            k = kern_ref[x, sl, :]
            re[x] = re[x] * k
            im[x] = im[x] * k
        im, re = fft_list(im, re)
        for x in range(n):
            a, b = re[x], im[x]
            if x:
                c, s = tw_ref[0, x : x + 1, :], tw_ref[1, x : x + 1, :]
                a, b = a * c - b * s, b * c + a * s
            vre[x, sl, :] = a * sign + swap(a)
            vim[x, sl, :] = b * sign + swap(b)
        return carry

    lax.fori_loop(0, rows // sub, x_body, 0)
    each_part(inverse)


def apply_pair(spots, mine, other, orbital, kern):
    share, rows, lanes = mine[0].shape
    last, row, tw = transform_tables(rows)
    shape = jax.ShapeDtypeStruct(mine[0].shape, jnp.float32)
    vm = pl.BlockSpec(memory_space=pltpu.VMEM)
    operands = [*mine, *other, *orbital, kern, np.stack(last + row), tw]
    count = len(mine)
    outs = pl.pallas_call(
        pair_kernel,
        out_shape=(shape,) * (2 * count),
        in_specs=[pl.BlockSpec(memory_space=pltpu.SMEM)] + [vm] * len(operands),
        out_specs=(vm,) * (2 * count),
        scratch_shapes=[pltpu.VMEM((count * share, rows, lanes), jnp.float32)] * 2,
        cost_estimate=pl.CostEstimate(
            flops=2 * 10**9, bytes_accessed=7 * 2**20, transcendentals=0
        ),
        compiler_params=pltpu.CompilerParams(vmem_limit_bytes=30 * 2**20),
        name="pair",
    )(spots, *operands)
    return outs[:count], outs[count:]


LANES = 128


def intersect_kernel(slot_ref, bands_ref, chunk_ref, before_ref, out_ref, turned, sums):
    nbands, cells, lanes = bands_ref.shape
    sub, group = 8, 8
    low = lax.broadcasted_iota(jnp.int32, (cells, lanes), 1) < lanes // 2
    rolled = pltpu.roll(chunk_ref[...], lanes // 2, 1)
    turned[...] = jnp.where(low, rolled, -rolled)
    for first in range(0, nbands, group):

        def body(t, acc):
            sl = pl.ds(pl.multiple_of(t * sub, sub), sub)
            real, imag = chunk_ref[sl, :], turned[sl, :]
            out = []
            for a in range(group):
                band = bands_ref[first + a, sl, :]
                out.append(acc[2 * a] + band * real)
                out.append(acc[2 * a + 1] + band * imag)
            return tuple(out)

        zero = jnp.zeros((sub, lanes), jnp.float32)
        acc = lax.fori_loop(0, cells // sub, body, (zero,) * (2 * group), unroll=4)
        for a in range(group):
            sums[first + a] = acc[2 * a]
            sums[nbands + first + a] = acc[2 * a + 1]
    column = lax.broadcasted_iota(jnp.int32, out_ref.shape, 1)
    value = jnp.sum(jnp.sum(sums[...], axis=1), axis=1, keepdims=True)
    out_ref[...] = before_ref[...] + jnp.where(column == slot_ref[0], value, 0.0)


def intersect(slot, bands, chunk, before):
    nbands, lanes = bands.shape[0], bands.shape[-1]
    bands = bands.reshape(nbands, -1, lanes)
    chunk = chunk.reshape(-1, lanes)
    vm = pl.BlockSpec(memory_space=pltpu.VMEM)
    return pl.pallas_call(
        intersect_kernel,
        out_shape=jax.ShapeDtypeStruct((2 * nbands, lanes), jnp.float32),
        in_specs=[pl.BlockSpec(memory_space=pltpu.SMEM), vm, vm, vm],
        out_specs=vm,
        scratch_shapes=[
            pltpu.VMEM(chunk.shape, jnp.float32),
            pltpu.VMEM((2 * nbands, 8, lanes), jnp.float32),
        ],
        cost_estimate=pl.CostEstimate(flops=10**7, bytes_accessed=4 * 2**20, transcendentals=0),
        compiler_params=pltpu.CompilerParams(vmem_limit_bytes=12 * 2**20),
        name="intersect",
    )(slot, bands, chunk, before)


def owner_kernel_values(path_point, mesh_point, shift, points):
    half = points // 2
    offset = (path_point - mesh_point).astype(jnp.float32) / KDIV
    lane = jnp.arange(2 * points, dtype=jnp.int32)

    def square(indices, axis):
        freqs = signed_frequencies(indices - shift[axis], points).astype(jnp.float32)
        return (freqs + offset[axis]) ** 2

    x_index = 2 * jnp.arange(half, dtype=jnp.int32)[:, None] + lane[None, :] // points
    plane = square(x_index, 0) + square(lane % points, 2)[None, :]
    rows = square(jnp.arange(points, dtype=jnp.int32), 1)
    squares = plane[:, None, :] + rows[None, :, None]
    scale = -MIXING * 4.0 * math.pi / float(points**3)
    return scale / ((2.0 * math.pi / BOX_LENGTH) ** 2 * squares + SCREEN_SQ)


def owner_body(path_bands, occupied, path_kpts, mesh_kpts, mesh_shift):
    points = path_bands.shape[3]
    nbands = path_bands.shape[1]
    share = path_bands.shape[2]
    grid_count = lax.axis_size("grid")
    mesh_count = lax.axis_size("mesh")
    path_count = lax.axis_size("path")
    grid_index = lax.axis_index("grid")
    mesh_index = lax.axis_index("mesh")
    path_index = lax.axis_index("path")
    core = grid_index & 1
    z = grid_index >> 1
    nz = grid_count // 2
    column_bands = nbands // mesh_count
    rounds = column_bands // nz
    bands = path_bands[0]
    offsets = (2, 3, 1)

    def grid_swap(value, mask):
        return lax.ppermute(value, "grid", [(i, i ^ mask) for i in range(grid_count)])

    def axis_swap(value, axis, count):
        return lax.ppermute(value, axis, [(i, i ^ 1) for i in range(count)])

    piece = occupied[0, 0]
    got = {0: piece}
    for d in offsets:
        got[d] = grid_swap(piece, 2 * d)
    first = jnp.stack([got[0], got[1]])
    second = jnp.stack([got[2], got[3]])
    same = mesh_index == core

    def by_orbital(mine):
        theirs = axis_swap(mine, "mesh", mesh_count)
        kept = jnp.where(same, mine, theirs)
        crossed = grid_swap(jnp.where(same, theirs, mine), 1)
        return kept, crossed

    first_own = jnp.stack(by_orbital(first))
    first_far = axis_swap(first_own, "path", path_count)
    rows = jnp.stack([second, axis_swap(second, "path", path_count)])
    orbital = (first_own, first_far, *by_orbital(rows))

    mesh_point = lax.dynamic_index_in_dim(mesh_kpts, core, 0, keepdims=False)
    shift = lax.dynamic_index_in_dim(mesh_shift, core, 0, keepdims=False)
    kernel = owner_kernel_values(path_kpts[0], mesh_point, shift, points)
    spots = jnp.stack([z, core, path_index])

    received = []
    for turn in range(rounds):
        parts = [None] * nz
        for d in (0,) + offsets:
            at = mesh_index * column_bands + rounds * (z ^ d) + turn
            sent = lax.dynamic_index_in_dim(bands, at, 0, keepdims=False)
            parts[d] = grid_swap(sent, 2 * d) if d else sent
        received.append(parts)

    result = jnp.zeros((column_bands, share, points, 2 * points), jnp.float32)
    inner = jnp.zeros((2 * nbands, 2 * points), jnp.float32)
    for turn in range(rounds):
        mine = received[turn]
        other = [grid_swap(mine[d], 1) for d in range(nz)]
        keep, send = apply_pair(spots, mine, other, orbital, kernel)
        chunks = {}
        for d in offsets + (0,):
            chunk = keep[d] + grid_swap(send[d], 1)
            chunks[d] = grid_swap(chunk, 2 * d) if d else chunk
        for d in (0, 1, 2, 3):
            slot = rounds * (z ^ d) + turn
            result = lax.dynamic_update_index_in_dim(result, chunks[d], slot, 0)
            at = (mesh_index * column_bands + slot).reshape(1)
            inner = intersect(at, bands, chunks[d], inner)
    for bit in range(grid_count.bit_length() - 1):
        inner = inner + grid_swap(inner, 1 << bit)
    inner = inner + axis_swap(inner, "mesh", mesh_count)
    intersection = inner[:, :nbands].reshape(2, nbands, nbands) / float(points**3)
    return (result[None], intersection[None])


def owner_per_device(*operands):
    return owner_body(*operands)


def owner_fits(mesh, path_bands, occupied):
    paths, columns, planes = mesh.shape["path"], mesh.shape["mesh"], mesh.shape["grid"]
    points, nbands = path_bands.shape[3], path_bands.shape[1]
    orbitals = occupied.shape[0] * occupied.shape[1]
    return (
        paths == 2
        and columns == 2
        and planes == 8
        and path_bands.shape[0] == paths
        and occupied.shape[0] == columns
        and orbitals == columns
        and 2 * points == LANES
        and path_bands.shape[2] == points
        and nbands % (columns * planes // 2) == 0
        and points % (4 * planes) == 0
    )


def solution(mesh):
    def run(path_bands, occupied, path_kpts, mesh_kpts, mesh_shift):
        fits = owner_fits(mesh, path_bands, occupied)
        step = jax.shard_map(
            owner_per_device if fits else spread_per_device,
            mesh=mesh,
            in_specs=(
                P("path", None, "grid", None, None),
                P("mesh", None, "grid", "path", None),
                P("path", None),
                P(),
                P(),
            ),
            out_specs=(P("path", "mesh", "grid", None, None), P("path", None, None, None)),
            check_vma=False,
        )
        return step(path_bands, occupied, path_kpts, mesh_kpts, mesh_shift)

    return run
```

```python
import math

import jax
import jax.numpy as jnp
import ml_dtypes
import numpy as np
from jax import lax
from jax.experimental import pallas as pl
from jax.experimental.pallas import tpu as pltpu
from jax.sharding import PartitionSpec as P

KDIV = 8


BOX_LENGTH = 42.7
SCREEN_SQ = 0.04
MIXING = 0.25
HIGHEST_PRECISION = lax.Precision.HIGHEST


def signed_frequencies(indices, points):
    return (indices + points // 2) % points - points // 2


def dft_tables(positions, points):
    freqs = jnp.arange(points, dtype=jnp.int32)
    product = positions[:, None] * freqs[None, :] % points
    angles = 2.0 * math.pi / points * product.astype(jnp.float32)
    return (jnp.cos(angles), jnp.sin(angles))


def last_matrix(points, inverse):
    cosine_table, sine_table = dft_tables(jnp.arange(points, dtype=jnp.int32), points)
    if inverse:
        upper = jnp.concatenate([cosine_table, sine_table], 1)
        lower = jnp.concatenate([-sine_table, cosine_table], 1)
    else:
        upper = jnp.concatenate([cosine_table, -sine_table], 1)
        lower = jnp.concatenate([sine_table, cosine_table], 1)
    return jnp.concatenate([upper, lower], 0)


def along_axis(values, cosine_table, sine_table, contract_dim, inverse):
    letters = "abcde"
    form = (
        letters
        + ","
        + letters[contract_dim]
        + "w->"
        + letters[:contract_dim]
        + "w"
        + letters[contract_dim + 1 :]
    )
    cos_part = jnp.einsum(form, values, cosine_table, precision=HIGHEST_PRECISION)
    sin_part = jnp.einsum(form, values, sine_table, precision=HIGHEST_PRECISION)
    half_width = values.shape[-1] // 2
    sin_real = sin_part[..., :half_width]
    sin_imag = sin_part[..., half_width:]
    if inverse:
        return cos_part + jnp.concatenate([-sin_imag, sin_real], -1)
    return cos_part + jnp.concatenate([sin_imag, -sin_real], -1)


def rotate_orbitals(orbitals, shifts, x_planes):
    points = orbitals.shape[3]
    coords = jnp.arange(points, dtype=jnp.int32)
    product = (
        shifts[:, 0][:, None, None, None] * x_planes[None, :, None, None]
        + shifts[:, 1][:, None, None, None] * coords[None, None, :, None]
        + shifts[:, 2][:, None, None, None] * coords[None, None, None, :]
    ) % points
    angles = 2.0 * math.pi / points * product.astype(jnp.float32)
    cosines = jnp.cos(angles)[:, None]
    sines = jnp.sin(angles)[:, None]
    real_part = orbitals[..., :points]
    imag_part = orbitals[..., points:]
    return jnp.concatenate(
        [real_part * cosines - imag_part * sines, real_part * sines + imag_part * cosines], -1
    )


def pair_fields(rotated, band_fields):
    points = band_fields.shape[2]
    rot_real = rotated[..., :points][:, :, None]
    rot_imag = rotated[..., points:][:, :, None]
    band_real = band_fields[..., :points][None, None]
    band_imag = band_fields[..., points:][None, None]
    pairs = jnp.concatenate(
        [rot_real * band_real + rot_imag * band_imag, rot_real * band_imag - rot_imag * band_real],
        -1,
    )
    return pairs.reshape(
        (rotated.shape[0], rotated.shape[1] * band_fields.shape[0]) + band_fields.shape[1:]
    )


def accumulate(rotated, potential, nbands):
    points = rotated.shape[3]
    shaped = potential.reshape((rotated.shape[0], rotated.shape[1], nbands) + potential.shape[2:])
    rot_real = rotated[..., :points][:, :, None]
    rot_imag = rotated[..., points:][:, :, None]
    pot_real = shaped[..., :points]
    pot_imag = shaped[..., points:]
    summed = jnp.concatenate(
        [
            jnp.sum(rot_real * pot_real - rot_imag * pot_imag, axis=(0, 1)),
            jnp.sum(rot_real * pot_imag + rot_imag * pot_real, axis=(0, 1)),
        ],
        -1,
    )
    return -MIXING * summed


def intersection_part(band_fields, applied):
    points = band_fields.shape[2]
    nbands = band_fields.shape[0]
    band_real = band_fields[..., :points].reshape(nbands, -1)
    band_imag = band_fields[..., points:].reshape(nbands, -1)
    app_real = applied[..., :points].reshape(applied.shape[0], -1)
    app_imag = applied[..., points:].reshape(applied.shape[0], -1)
    real_sum = jnp.dot(band_real, app_real.T, precision=HIGHEST_PRECISION) + jnp.dot(
        band_imag, app_imag.T, precision=HIGHEST_PRECISION
    )
    imag_sum = jnp.dot(band_real, app_imag.T, precision=HIGHEST_PRECISION) - jnp.dot(
        band_imag, app_real.T, precision=HIGHEST_PRECISION
    )
    return jnp.stack([real_sum, imag_sum]) / float(points**3)


def screened_kernel(path_point, mesh_points, y_rows, points):
    offset_frac = (path_point[None, :] - mesh_points).astype(jnp.float32) / KDIV
    all_freqs = signed_frequencies(jnp.arange(points, dtype=jnp.int32), points).astype(jnp.float32)
    row_freqs = signed_frequencies(y_rows, points).astype(jnp.float32)
    square_x = (all_freqs[None, :] + offset_frac[:, 0:1]) ** 2
    square_y = (row_freqs[None, :] + offset_frac[:, 1:2]) ** 2
    square_z = (all_freqs[None, :] + offset_frac[:, 2:3]) ** 2
    squares = square_x[:, :, None, None] + square_y[:, None, :, None] + square_z[:, None, None, :]
    kernel = (
        4.0 * math.pi / ((2.0 * math.pi / BOX_LENGTH) ** 2 * squares + SCREEN_SQ) / float(points**3)
    )
    return jnp.concatenate([kernel, kernel], -1)


def spread_per_device(path_bands, occupied, path_kpts, mesh_kpts, mesh_shift):
    points = path_bands.shape[3]
    nbands = path_bands.shape[1]
    local_planes = path_bands.shape[2]
    grid_count = lax.axis_size("grid")
    mesh_count = lax.axis_size("mesh")
    grid_index = lax.axis_index("grid")
    mesh_index = lax.axis_index("mesh")
    whole_orbitals = lax.all_gather(occupied, "path", axis=3, tiled=True)
    forward_z = last_matrix(points, False)
    inverse_z = last_matrix(points, True)
    cos_y, sin_y = dft_tables(jnp.arange(points, dtype=jnp.int32), points)
    band_all = path_bands[0]
    path_point = path_kpts[0]
    share_planes = local_planes // mesh_count
    both_orbitals = lax.all_to_all(whole_orbitals, "mesh", split_axis=2, concat_axis=0, tiled=True)
    x_planes = (
        grid_index * local_planes
        + mesh_index * share_planes
        + jnp.arange(share_planes, dtype=jnp.int32)
    )
    rotated = rotate_orbitals(both_orbitals, mesh_shift, x_planes)
    band_mine = lax.dynamic_slice_in_dim(band_all, mesh_index * share_planes, share_planes, 1)
    values = pair_fields(rotated, band_mine)
    values = jnp.matmul(values, forward_z, precision=HIGHEST_PRECISION)
    pair_field = along_axis(values, cos_y, sin_y, 3, False)
    wide_count = mesh_count * grid_count
    rows_y = points // wide_count
    flat_index = mesh_index * grid_count + grid_index
    y_rows = flat_index * rows_y + jnp.arange(rows_y, dtype=jnp.int32)
    kernel = screened_kernel(path_point, mesh_kpts, y_rows, points)
    positions = jnp.arange(points, dtype=jnp.int32)
    piece_index = positions // share_planes
    plane_index = (
        piece_index % grid_count * local_planes
        + piece_index // grid_count * share_planes
        + positions % share_planes
    )
    cos_x, sin_x = dft_tables(plane_index, points)
    moved = (
        along_axis(
            lax.all_to_all(pair_field, ("mesh", "grid"), split_axis=3, concat_axis=2, tiled=True),
            cos_x,
            sin_x,
            2,
            False,
        )
        * kernel[:, None]
    )
    moved = along_axis(moved, cos_x.T, sin_x.T, 2, True)
    potential = lax.all_to_all(moved, ("mesh", "grid"), split_axis=2, concat_axis=3, tiled=True)
    values = potential
    values = along_axis(values, cos_y, sin_y, 3, True)
    applied = accumulate(
        rotated, jnp.matmul(values, inverse_z, precision=HIGHEST_PRECISION), nbands
    )
    partial_value = intersection_part(band_mine, applied)
    result_bands = lax.all_to_all(applied, "mesh", split_axis=0, concat_axis=1, tiled=True)
    intersection = lax.psum(partial_value, ("mesh", "grid"))
    return (result_bands[None], intersection[None])


def split_table(table):
    high = table.astype(ml_dtypes.bfloat16)
    low = (table - high.astype(np.float64)).astype(ml_dtypes.bfloat16)
    return high, low


def transform_tables(points):
    index = np.arange(points)
    angles = 2.0 * np.pi * ((index[:, None] * index[None, :]) % points) / points
    cos, sin = np.cos(angles), np.sin(angles)
    zero = np.zeros_like(cos)
    last_forward = np.block([[cos, zero, -sin, zero], [sin, zero, cos, zero], [zero, cos, zero, -sin], [zero, sin, zero, cos]])
    last_inverse = np.block([[cos, sin, zero, zero], [zero, zero, cos, sin], [-sin, cos, zero, zero], [zero, zero, -sin, cos]])
    row_forward = np.block([[cos, sin], [-sin, cos]])
    row_inverse = np.block([[cos, -sin], [sin, cos]])
    last = []
    for table in (last_forward, last_inverse):
        last.extend(split_table(table))
    rows = []
    for table in (row_forward, row_inverse):
        high, low = split_table(table)
        rows.append(np.block([[high, high], [low, np.zeros_like(low)]]).astype(ml_dtypes.bfloat16))
    half = points // 2
    turn = 2.0 * np.pi * np.arange(half) / points
    ones = np.ones((half, points))
    twiddle = np.stack([np.concatenate([ones, ones * np.cos(turn)[:, None]], 1), np.concatenate([0 * ones, ones * np.sin(turn)[:, None]], 1)])
    return last, rows, twiddle.astype(np.float32)


def split_values(values):
    high = values.astype(jnp.bfloat16)
    low = (values - high.astype(jnp.float32)).astype(jnp.bfloat16)
    return high, low


def fft_list(real, imag):
    size = len(real)
    if size == 1:
        return real, imag
    half = size // 2
    even_r, even_i = fft_list(real[0::2], imag[0::2])
    odd_r, odd_i = fft_list(real[1::2], imag[1::2])
    out_r, out_i = [None] * size, [None] * size
    root = math.sqrt(0.5)
    for k in range(half):
        r, i = odd_r[k], odd_i[k]
        if k == 0:
            tr, ti = r, i
        elif 4 * k == size:
            tr, ti = i, -r
        elif 8 * k == size:
            tr, ti = (r + i) * root, (i - r) * root
        elif 8 * k == 3 * size:
            tr, ti = (i - r) * root, (r + i) * (-root)
        else:
            c, s = math.cos(2 * math.pi * k / size), math.sin(2 * math.pi * k / size)
            tr, ti = r * c + i * s, i * c - r * s
        if 4 * k == size:
            out_r[k], out_i[k] = even_r[k] + i, even_i[k] - r
            out_r[k + half], out_i[k + half] = even_r[k] - i, even_i[k] + r
        else:
            out_r[k], out_i[k] = even_r[k] + tr, even_i[k] + ti
            out_r[k + half], out_i[k + half] = even_r[k] - tr, even_i[k] - ti
    return out_r, out_i


def f32dot(a, b):
    return jnp.dot(a, b, preferred_element_type=jnp.float32)


def pair_kernel(spots_ref, *refs):
    nz = 4
    mine, other = refs[:nz], refs[nz : 2 * nz]
    first_own, first_far, second_kept, second_crossed = refs[2 * nz : 2 * nz + 4]
    kern_ref, tw_ref, table_hbm = refs[2 * nz + 4 : 2 * nz + 7]
    keep, send = refs[2 * nz + 7 : 3 * nz + 7], refs[3 * nz + 7 : 4 * nz + 7]
    vre, vim, table_ref, sem = refs[4 * nz + 7 :]
    copy = pltpu.make_async_copy(table_hbm, table_ref, sem)
    copy.start()
    lfh, lfl, lih, lil, rf, ri = [table_ref.at[at] for at in range(6)]
    share, rows, lanes = mine[0].shape
    points = rows
    half_z = nz // 2
    z, core, path = spots_ref[0], spots_ref[1], spots_ref[2]
    low = lax.broadcasted_iota(jnp.int32, (rows, lanes), 1) < points
    step = 8

    def swap(v):
        return pltpu.roll(v, points, v.ndim - 1)

    def orbital(d, parity, i):
        at = d // 2
        if d % 2 == 0:
            own, far = first_own[parity, at, i], first_far[parity, at, i]
        else:
            ref = second_crossed if parity else second_kept
            r = jnp.concatenate([ref[path, at, i], ref[1 - path, at, i]], 0)
            s = swap(r)
            return jnp.where(low, r, s), jnp.where(low, s, -r)
        r = jnp.concatenate([jnp.where(path == 0, own, far), jnp.where(path == 0, far, own)], 0)
        s = swap(r)
        return jnp.where(low, r, s), jnp.where(low, s, -r)

    def place(d, parity, part):
        side = core if parity == 0 else 1 - core
        return share * (2 * ((z ^ d) & 1) + side) + part * step

    def forward(d, parity, part):
        first = place(d, parity, part)
        halves = []
        for at in (d, d ^ half_z):
            planes = []
            for i in range(step):
                real, imag = orbital(at, parity, part * step + i)
                band = (other if parity else mine)[at][part * step + i]
                planes.append(real * band + imag * swap(band))
            halves.append(jnp.concatenate(planes, 0))
        hi, lo = split_values(jnp.concatenate(halves, 1))
        u = f32dot(hi, lfh[...]) + f32dot(lo, lfh[...]) + f32dot(hi, lfl[...])
        uh, ul = split_values(u)
        for i in range(0, step, 2):

            def stack(v):
                cols = []
                for j in (0, 1):
                    plane = v[(i + j) * rows : (i + j + 1) * rows]
                    cols.append(jnp.concatenate([plane[:, :lanes], plane[:, lanes:]], 0))
                return jnp.concatenate(cols, 1)

            d2 = f32dot(rf[...], jnp.concatenate([stack(uh), stack(ul)], 0))
            v = d2[: 2 * rows] + d2[2 * rows :]
            for j in (0, 1):
                vre[first + i + j] = v[:rows, j * lanes : (j + 1) * lanes]
                vim[first + i + j] = v[rows:, j * lanes : (j + 1) * lanes]

    def inverse(d, parity, part):
        first = place(d, parity, part)
        res = []
        for i in range(0, step, 2):
            cols = []
            for j in (0, 1):
                rh, rl = split_values(vre[first + i + j])
                ih, il = split_values(vim[first + i + j])
                cols.append(jnp.concatenate([rh, ih, rl, il], 0))
            d2 = f32dot(ri[...], jnp.concatenate(cols, 1))
            u = d2[: 2 * rows] + d2[2 * rows :]
            for j in (0, 1):
                plane = u[:, j * lanes : (j + 1) * lanes]
                res.append(jnp.concatenate([plane[:rows], plane[rows:]], 1))
        hi, lo = split_values(jnp.concatenate(res, 0))
        p = f32dot(hi, lih[...]) + f32dot(lo, lih[...]) + f32dot(hi, lil[...])
        for i in range(step):
            for side, at in enumerate((d, d ^ half_z)):
                real, imag = orbital(at, parity, part * step + i)
                pot = p[i * rows : (i + 1) * rows, side * lanes : (side + 1) * lanes]
                out = send if parity else keep
                out[at][part * step + i] = real * pot - imag * swap(pot)

    def each_part(work):
        def body(part, carry):
            for d in range(half_z):
                for parity in (0, 1):
                    work(d, parity, part)
            return carry

        lax.fori_loop(0, share // step, body, 0)

    copy.wait()
    each_part(forward)

    n = vre.shape[0]
    sub = 8
    sign = jnp.where(low[:sub], 1.0, -1.0).astype(jnp.float32)

    def x_body(t, carry):
        sl = pl.ds(pl.multiple_of(t * sub, sub), sub)
        re, im = [], []
        for x in range(n):
            a, b = vre[x, sl, :], vim[x, sl, :]
            a = a * sign + swap(a)
            b = b * sign + swap(b)
            if x:
                c, s = tw_ref[0, x : x + 1, :], tw_ref[1, x : x + 1, :]
                a, b = a * c + b * s, b * c - a * s
            re.append(a)
            im.append(b)
        re, im = fft_list(re, im)
        for x in range(n):
            k = kern_ref[x, sl, :]
            re[x] = re[x] * k
            im[x] = im[x] * k
        im, re = fft_list(im, re)
        for x in range(n):
            a, b = re[x], im[x]
            if x:
                c, s = tw_ref[0, x : x + 1, :], tw_ref[1, x : x + 1, :]
                a, b = a * c - b * s, b * c + a * s
            vre[x, sl, :] = a * sign + swap(a)
            vim[x, sl, :] = b * sign + swap(b)
        return carry

    lax.fori_loop(0, rows // sub, x_body, 0)
    each_part(inverse)


def apply_pair(spots, mine, other, orbital, kern):
    share, rows, lanes = mine[0].shape
    last, row, tw = transform_tables(rows)
    shape = jax.ShapeDtypeStruct(mine[0].shape, jnp.float32)
    vm = pl.BlockSpec(memory_space=pltpu.VMEM)
    table = jnp.asarray(np.stack(last + row))
    operands = [*mine, *other, *orbital, kern, tw]
    count = len(mine)
    outs = pl.pallas_call(
        pair_kernel,
        out_shape=(shape,) * (2 * count),
        in_specs=[pl.BlockSpec(memory_space=pltpu.SMEM)]
        + [vm] * len(operands)
        + [pl.BlockSpec(memory_space=pltpu.HBM)],
        out_specs=(vm,) * (2 * count),
        scratch_shapes=[pltpu.VMEM((count * share, rows, lanes), jnp.float32)] * 2
        + [pltpu.VMEM(table.shape, table.dtype), pltpu.SemaphoreType.DMA],
        cost_estimate=pl.CostEstimate(
            flops=2 * 10**9, bytes_accessed=7 * 2**20, transcendentals=0
        ),
        compiler_params=pltpu.CompilerParams(vmem_limit_bytes=30 * 2**20),
        name="pair",
    )(spots, *operands, table)
    return outs[:count], outs[count:]


LANES = 128


def intersect_kernel(slot_ref, bands_ref, chunk_ref, before_ref, out_ref, turned, sums):
    nbands, cells, lanes = bands_ref.shape
    sub, group = 8, 8
    low = lax.broadcasted_iota(jnp.int32, (cells, lanes), 1) < lanes // 2
    rolled = pltpu.roll(chunk_ref[...], lanes // 2, 1)
    turned[...] = jnp.where(low, rolled, -rolled)
    for first in range(0, nbands, group):

        def body(t, acc):
            sl = pl.ds(pl.multiple_of(t * sub, sub), sub)
            real, imag = chunk_ref[sl, :], turned[sl, :]
            out = []
            for a in range(group):
                band = bands_ref[first + a, sl, :]
                out.append(acc[2 * a] + band * real)
                out.append(acc[2 * a + 1] + band * imag)
            return tuple(out)

        zero = jnp.zeros((sub, lanes), jnp.float32)
        acc = lax.fori_loop(0, cells // sub, body, (zero,) * (2 * group), unroll=4)
        for a in range(group):
            sums[first + a] = acc[2 * a]
            sums[nbands + first + a] = acc[2 * a + 1]
    column = lax.broadcasted_iota(jnp.int32, out_ref.shape, 1)
    value = jnp.sum(jnp.sum(sums[...], axis=1), axis=1, keepdims=True)
    out_ref[...] = before_ref[...] + jnp.where(column == slot_ref[0], value, 0.0)


def intersect(slot, bands, chunk, before):
    nbands, lanes = bands.shape[0], bands.shape[-1]
    bands = bands.reshape(nbands, -1, lanes)
    chunk = chunk.reshape(-1, lanes)
    vm = pl.BlockSpec(memory_space=pltpu.VMEM)
    return pl.pallas_call(
        intersect_kernel,
        out_shape=jax.ShapeDtypeStruct((2 * nbands, lanes), jnp.float32),
        in_specs=[pl.BlockSpec(memory_space=pltpu.SMEM), vm, vm, vm],
        out_specs=vm,
        scratch_shapes=[
            pltpu.VMEM(chunk.shape, jnp.float32),
            pltpu.VMEM((2 * nbands, 8, lanes), jnp.float32),
        ],
        cost_estimate=pl.CostEstimate(flops=10**7, bytes_accessed=4 * 2**20, transcendentals=0),
        compiler_params=pltpu.CompilerParams(vmem_limit_bytes=12 * 2**20),
        name="intersect",
    )(slot, bands, chunk, before)


def owner_kernel_values(path_point, mesh_point, shift, points):
    half = points // 2
    offset = (path_point - mesh_point).astype(jnp.float32) / KDIV
    lane = jnp.arange(2 * points, dtype=jnp.int32)

    def square(indices, axis):
        freqs = signed_frequencies(indices - shift[axis], points).astype(jnp.float32)
        return (freqs + offset[axis]) ** 2

    x_index = 2 * jnp.arange(half, dtype=jnp.int32)[:, None] + lane[None, :] // points
    plane = square(x_index, 0) + square(lane % points, 2)[None, :]
    rows = square(jnp.arange(points, dtype=jnp.int32), 1)
    squares = plane[:, None, :] + rows[None, :, None]
    scale = -MIXING * 4.0 * math.pi / float(points**3)
    return scale / ((2.0 * math.pi / BOX_LENGTH) ** 2 * squares + SCREEN_SQ)


def owner_body(path_bands, occupied, path_kpts, mesh_kpts, mesh_shift):
    points = path_bands.shape[3]
    nbands = path_bands.shape[1]
    share = path_bands.shape[2]
    grid_count = lax.axis_size("grid")
    mesh_count = lax.axis_size("mesh")
    path_count = lax.axis_size("path")
    grid_index = lax.axis_index("grid")
    mesh_index = lax.axis_index("mesh")
    path_index = lax.axis_index("path")
    core = grid_index & 1
    z = grid_index >> 1
    nz = grid_count // 2
    column_bands = nbands // mesh_count
    rounds = column_bands // nz
    bands = path_bands[0]
    offsets = (2, 3, 1)

    def grid_swap(value, mask):
        return lax.ppermute(value, "grid", [(i, i ^ mask) for i in range(grid_count)])

    def axis_swap(value, axis, count):
        return lax.ppermute(value, axis, [(i, i ^ 1) for i in range(count)])

    piece = occupied[0, 0]
    first = jnp.stack([piece, grid_swap(piece, 2 * 2)])
    second = grid_swap(first, 2)
    same = mesh_index == core

    def by_orbital(mine):
        theirs = axis_swap(mine, "mesh", mesh_count)
        kept, crossed = jnp.where(same, mine, theirs), jnp.where(same, theirs, mine)
        return kept, grid_swap(crossed, 1)

    first_own = jnp.stack(by_orbital(first))
    first_far = axis_swap(first_own, "path", path_count)
    rows = jnp.stack([second, axis_swap(second, "path", path_count)])
    orbital = (first_own, first_far, *by_orbital(rows))

    mesh_point = lax.dynamic_index_in_dim(mesh_kpts, core, 0, keepdims=False)
    shift = lax.dynamic_index_in_dim(mesh_shift, core, 0, keepdims=False)
    kernel = owner_kernel_values(path_kpts[0], mesh_point, shift, points)
    spots = jnp.stack([z, core, path_index])

    received = []
    for turn in range(rounds):
        parts = [None] * nz
        for d in (0,) + offsets:
            at = mesh_index * column_bands + rounds * (z ^ d) + turn
            sent = lax.dynamic_index_in_dim(bands, at, 0, keepdims=False)
            parts[d] = grid_swap(sent, 2 * d) if d else sent
        received.append(parts)

    result = jnp.zeros((column_bands, share, points, 2 * points), jnp.float32)
    inner = jnp.zeros((2 * nbands, 2 * points), jnp.float32)
    for turn in range(rounds):
        mine = received[turn]
        other = [grid_swap(mine[d], 1) for d in range(nz)]
        keep, send = apply_pair(spots, mine, other, orbital, kernel)
        chunks = {}
        for d in offsets + (0,):
            crossed = grid_swap(send[d], 1)
            chunk = keep[d] + crossed
            chunks[d] = grid_swap(chunk, 2 * d) if d else chunk
        for d in (0, 1, 2, 3):
            slot = rounds * (z ^ d) + turn
            result = lax.dynamic_update_index_in_dim(result, chunks[d], slot, 0)
            at = (mesh_index * column_bands + slot).reshape(1)
            inner = intersect(at, bands, chunks[d], inner)

    def chip_swap(value, mask):
        axes, count = ("mesh", "grid"), mesh_count * grid_count
        return lax.ppermute(value, axes, [(i, i ^ mask) for i in range(count)])

    far = [grid_swap(inner, 2 * d) for d in (3, 2, 1)]
    inner = (inner + far[2]) + (far[0] + far[1])
    near = [chip_swap(inner, mask) for mask in (grid_count, grid_count + 1, 1)]
    inner = (inner + near[2]) + (near[0] + near[1])
    intersection = inner[:, :nbands].reshape(2, nbands, nbands) / float(points**3)
    return (result[None], intersection[None])


def owner_per_device(*operands):
    return owner_body(*operands)


def owner_fits(mesh, path_bands, occupied):
    paths, columns, planes = mesh.shape["path"], mesh.shape["mesh"], mesh.shape["grid"]
    points, nbands = path_bands.shape[3], path_bands.shape[1]
    orbitals = occupied.shape[0] * occupied.shape[1]
    return (
        paths == 2
        and columns == 2
        and planes == 8
        and path_bands.shape[0] == paths
        and occupied.shape[0] == columns
        and orbitals == columns
        and 2 * points == LANES
        and path_bands.shape[2] == points
        and nbands % (columns * planes // 2) == 0
        and points % (4 * planes) == 0
    )


def solution(mesh):
    def run(path_bands, occupied, path_kpts, mesh_kpts, mesh_shift):
        fits = owner_fits(mesh, path_bands, occupied)
        step = jax.shard_map(
            owner_per_device if fits else spread_per_device,
            mesh=mesh,
            in_specs=(
                P("path", None, "grid", None, None),
                P("mesh", None, "grid", "path", None),
                P("path", None),
                P(),
                P(),
            ),
            out_specs=(P("path", "mesh", "grid", None, None), P("path", None, None, None)),
            check_vma=False,
        )
        return step(path_bands, occupied, path_kpts, mesh_kpts, mesh_shift)

    return run
```
